512 devices in a mesh: row: 8 (over z), col: 16 (over y, core), vox: 4 (over x).
Axes of the slice: x: 4, y: 8, z: 8, core: 2. Of those that a mesh axis runs over, the one named last changes fastest.
Arguments:
- panel_top: bfloat16 [1024, 1024], P('row', ('col', 'vox')), may hold values from -0.059814453 to 0.059814453
- panel_low: bfloat16 [8192, 1024], P('row', ('col', 'vox')), may hold values from -1.1953125 to 1.1953125
- panel_next: bfloat16 [8192, 1024], P('row', ('col', 'vox')), may hold values from -1.1953125 to 1.1953125
- gram_rest: bfloat16 [8192, 8192], P('row', ('col', 'vox')), may hold values from -18 to 18
- inverses: bfloat16 [2, 1024, 1024], P(None, 'row'), as said below
- right_top: bfloat16 [2, 1024, 8192], P(None, None, ('col', 'vox')), may hold values from -1.796875 to 1.796875
- right_low: bfloat16 [8192, 8192], P('row', ('col', 'vox')), may hold values from -24 to 24
Outputs:
- factor: bfloat16 [2, 8192, 1024], P(None, 'row', ('col', 'vox'))
- solved: bfloat16 [2, 1024, 8192], P(None, None, ('col', 'vox'))
- trailing: float32 [8192, 8192], P('row', ('col', 'vox'))
- residual: float32 [8192, 8192], P('row', ('col', 'vox'))
The draws below stay inside these ranges and needn't reach their ends.
Inputs may be any that keep to these rules, and one draw needn't show every extreme that they name: Each inverses[k] is lower triangular with diagonal entries from 1 to 2.
All inputs are finite; a program needn't handle non-finite values.
Results may differ from the reference program's by a relative error of at most 0.0057.
Values may be sent and summed in bfloat16 or wider, within the bound.
No kernel may reach another device: no remote copies, remote signals or barrier semaphores. Data moves between devices by JAX's collectives and lax.ppermute only.
A program may use at most 64 MiB of HBM per device.

```python
import math
import jax
import jax.numpy as jnp
from jax import lax

PANEL = 1024
LOW = 8192
VOXELS = 8192


def draw_inverses(key, part):
    key_diag = jax.random.fold_in(key, 11)
    key_lower = jax.random.fold_in(key, 23)
    diagonal = jax.random.uniform(key_diag, (2, PANEL), jnp.float32, 1.0, 2.0)
    lower = jax.random.normal(key_lower, (2, PANEL, PANEL), jnp.float32)
    lower = jnp.tril(lower, -1) * (1.0 / math.sqrt(PANEL))
    identity = jnp.eye(PANEL, dtype=jnp.float32)
    whole = lower + identity[None, :, :] * diagonal[:, None, :]
    return whole.astype(jnp.bfloat16)


def block_scale(key, shape, cuts, low, high):
    def one(axis_at, blocks):
        heights = jax.random.uniform(jax.random.fold_in(jax.random.fold_in(key, 6), axis_at), (blocks,), jnp.float32, low / len(cuts), high / len(cuts))
        return jnp.repeat(jnp.exp(heights), shape[axis_at] // blocks).reshape((-1,) + (1,) * (len(shape) - axis_at - 1))

    level = one(*cuts[0])
    for cut in cuts[1:]:
        level = level * one(*cut)
    return level


def centred(own_key, extent, deviation, bound, cuts=(), held_as=jnp.bfloat16):
    level = block_scale(own_key, extent, cuts, -0.22, 0.18) if cuts else 1.0
    result = jax.random.normal(own_key, extent, jnp.float32) * deviation * level
    return jnp.minimum(jnp.maximum(result, -bound), bound).astype(held_as)


def setup_inputs(seed: int = 0) -> dict:
    splits = jax.random.split(jax.random.key(seed), 8)
    return {
        "panel_top": centred(splits[0], (PANEL, PANEL), 0.01, 0.059814453, ((0, 8), (1, 64))),
        "panel_low": centred(splits[1], (LOW, PANEL), 0.2, 1.1953125, ((0, 8), (1, 64))),
        "panel_next": centred(splits[2], (LOW, PANEL), 0.2, 1.1953125, ((0, 8), (1, 64))),
        "gram_rest": centred(splits[3], (LOW, LOW), 3.0, 18.0, ((0, 8), (1, 64))),
        "inverses": draw_inverses(jax.random.fold_in(splits[7], 71), 0),
        "right_top": centred(splits[5], (2, PANEL, VOXELS), 0.3, 1.796875, ((2, 64),)),
        "right_low": centred(splits[6], (LOW, VOXELS), 4.0, 24.0, ((0, 8), (1, 64))),
    }


def contract(left, right):
    return lax.dot_general(left, right, (((1,), (1,)), ((), ())), preferred_element_type=jnp.float32)


def reference(panel_top, panel_low, panel_next, gram_rest, inverses, right_top, right_low):
    inverse_one = inverses[0]
    inverse_two = inverses[1]
    first_top = contract(panel_top, inverse_one).astype(jnp.bfloat16)
    first_low = contract(panel_low, inverse_one).astype(jnp.bfloat16)
    updated = (panel_next.astype(jnp.float32) - contract(first_low, first_top)).astype(jnp.bfloat16)
    second_low = contract(updated, inverse_two).astype(jnp.bfloat16)
    first_solve = jnp.dot(inverse_one, right_top[0], preferred_element_type=jnp.float32).astype(jnp.bfloat16)
    top_new = (right_top[1].astype(jnp.float32) - jnp.dot(first_top, first_solve, preferred_element_type=jnp.float32)).astype(jnp.bfloat16)
    second_solve = jnp.dot(inverse_two, top_new, preferred_element_type=jnp.float32).astype(jnp.bfloat16)
    trailing = gram_rest.astype(jnp.float32) - contract(first_low, first_low) - contract(second_low, second_low)
    residual = right_low.astype(jnp.float32) - jnp.dot(first_low, first_solve, preferred_element_type=jnp.float32) - jnp.dot(second_low, second_solve, preferred_element_type=jnp.float32)
    factor = jnp.stack([first_low, second_low])
    solved = jnp.stack([first_solve, second_solve])
    return (factor, solved, trailing, residual)
```

```python
import jax
import jax.numpy as jnp
import numpy as np
from jax import lax
from jax.sharding import Mesh
from jax.sharding import PartitionSpec as P


def contract(left, right, dims):
    return lax.dot_general(left, right, (dims, ((), ())), preferred_element_type=jnp.float32)


def gather_small(block, axis, size):
    out = lax.all_to_all(jnp.tile(block, (size, 1)), axis, 0, 0, tiled=True)
    return out.reshape((size,) + block.shape)


def per_device(sizes, panel_top, panel_low, panel_next, gram_rest, inverses, right_top, right_low):
    rows, ys, cores, voxes = sizes
    axes = ("row", "y", "core", "vox")
    order = np.arange(rows * ys * cores * voxes).reshape(sizes)
    swap = list(zip(order.ravel().tolist(), order.transpose(1, 0, 2, 3).ravel().tolist()))
    y = lax.axis_index("y")
    core = lax.axis_index("core")
    vox = lax.axis_index("vox")
    width = panel_low.shape[1]
    rest_cols = gram_rest.shape[1]
    bf16 = jnp.bfloat16

    whole = lax.all_gather(inverses, "row", axis=1, tiled=True)
    top = gather_small(panel_top.T, "row", rows).transpose(1, 0, 2).reshape(width, -1)
    panels = jnp.stack([top, panel_low.T, panel_next.T])
    panels = lax.all_gather(panels, ("y", "core", "vox"), axis=1, tiled=True)

    low = panels[0:2].transpose(1, 0, 2).reshape(panels.shape[1], -1)
    first = contract(whole[0], low, ((1,), (0,))).astype(bf16)
    first_top, first_low = first[:, : panels.shape[2]], first[:, panels.shape[2] :]
    updated = (
        panels[2].astype(jnp.float32) - contract(first_top, first_low, ((0,), (0,)))
    ).astype(bf16)
    second_low = contract(whole[1], updated, ((1,), (0,))).astype(bf16)

    start = (core * voxes + vox) * rest_cols
    first_rows = lax.ppermute(lax.dynamic_slice_in_dim(first_low, start, rest_cols, 1), axes, swap)
    second_rows = lax.ppermute(lax.dynamic_slice_in_dim(second_low, start, rest_cols, 1), axes, swap)

    first_solve = contract(whole[0], right_top[0], ((1,), (0,))).astype(bf16)
    top_new = (
        right_top[1].astype(jnp.float32) - contract(first_top, first_solve, ((0,), (0,)))
    ).astype(bf16)
    second_solve = contract(whole[1], top_new, ((1,), (0,))).astype(bf16)

    residual = (
        right_low.astype(jnp.float32)
        - contract(first_low, first_solve, ((0,), (0,)))
        - contract(second_low, second_solve, ((0,), (0,)))
    )
    trailing = (
        gram_rest.astype(jnp.float32)
        - contract(first_low, first_rows, ((0,), (0,)))
        - contract(second_low, second_rows, ((0,), (0,)))
    )
    own = ((y * cores + core) * voxes + vox) * width
    factor = jnp.stack(
        [
            lax.dynamic_slice_in_dim(first_low, own, width, 0).T,
            lax.dynamic_slice_in_dim(second_low, own, width, 0).T,
        ]
    )
    solved = jnp.stack([first_solve, second_solve])
    return (factor, solved, trailing, residual)


def solution(mesh):
    cores = 2
    sizes = (mesh.shape["row"], mesh.shape["col"] // cores, cores, mesh.shape["vox"])
    split = Mesh(mesh.devices.reshape(sizes), ("row", "y", "core", "vox"))
    cols = ("y", "core", "vox")
    in_specs = (
        P("row", cols),
        P("row", cols),
        P("row", cols),
        P("row", cols),
        P(None, "row", None),
        P(None, None, cols),
        P("row", cols),
    )
    out_specs = (
        P(None, "row", cols),
        P(None, None, cols),
        P("row", cols),
        P("row", cols),
    )

    def body(*args):
        return per_device(sizes, *args)

    return jax.shard_map(body, mesh=split, in_specs=in_specs, out_specs=out_specs, check_vma=False)
```

```python
import functools

import jax
import jax.numpy as jnp
import numpy as np
from jax import lax
from jax.experimental import pallas as pl
from jax.experimental.pallas import tpu as pltpu
from jax.sharding import Mesh
from jax.sharding import PartitionSpec as P

TILE = 256


def factor_kernel(
    at_ref, inv_own, inv_other, panel_own, panel_other, side_one, side_two, gram, right,
    factor, solved, trailing, residual,
    inv, panels, side, top, first, updated, second, sems,
):
    z, core, own = at_ref[0], at_ref[1], at_ref[2]
    blocks = inv_own.shape[0]
    size = first.shape[0]
    f32, bf16 = jnp.float32, jnp.bfloat16

    inv_copies = []
    for i in range(blocks):
        spot = lax.rem(z + (blocks - i), blocks)
        for side_of, ref, half in ((0, inv_own, core), (1, inv_other, 1 - core)):
            inv_copies.append(
                pltpu.make_async_copy(ref.at[i], inv.at[half, spot], sems.at[2 * i + side_of])
            )
    panel_copies = []
    for p in range(panels.shape[0]):
        for side_of, ref, half in ((0, panel_own, core), (1, panel_other, 1 - core)):
            panel_copies.append(
                pltpu.make_async_copy(
                    ref.at[:, :, p],
                    panels.at[p, :, half],
                    sems.at[2 * blocks + 2 * p + side_of],
                )
            )
    side_copies = [
        pltpu.make_async_copy(side_one, side.at[0], sems.at[2 * blocks + 6]),
        pltpu.make_async_copy(side_two, side.at[1], sems.at[2 * blocks + 7]),
    ]
    for copy in inv_copies + panel_copies[:2] + panel_copies[2:4] + side_copies + panel_copies[4:]:
        copy.start()
    for copy in inv_copies:
        copy.wait()

    def inverse(k, i):
        rows = inv[k, 2 * i : 2 * i + 2].reshape(TILE, size)
        return rows[:, : (i + 1) * TILE]

    def lower(k, load, store):
        for i in range(size // TILE):
            store(i, jnp.dot(inverse(k, i), load((i + 1) * TILE), preferred_element_type=f32))

    def at(t):
        return pl.ds(pl.multiple_of(t * TILE, TILE), TILE)

    flat = panels.reshape(3, size, size)

    for copy in panel_copies[:2]:
        copy.wait()

    @pl.loop(0, size // TILE)
    def _(t):
        def store(i, x):
            top[at(t), i * TILE : (i + 1) * TILE] = x.astype(bf16).T

        lower(0, lambda n: flat[0, :n, at(t)], store)

    for copy in panel_copies[2:4] + side_copies:
        copy.wait()

    @pl.loop(0, size // TILE)
    def _(t):
        def store(i, x):
            first[i * TILE : (i + 1) * TILE, at(t)] = x.astype(bf16)

        lower(0, lambda n: flat[1, :n, at(t)], store)

    def store_side_one(i, x):
        first[i * TILE : (i + 1) * TILE, size:] = x.astype(bf16)

    lower(0, lambda n: side[0, :n, :], store_side_one)
    solved[0] = first[:, size + TILE // 2 :]

    for copy in panel_copies[4:]:
        copy.wait()

    def subtract(minuend, cols):
        for i in range(size // TILE):
            rows = slice(i * TILE, (i + 1) * TILE)
            change = jnp.dot(top[rows, :], first[:, cols], preferred_element_type=f32)
            updated[rows, cols] = (minuend(rows).astype(f32) - change).astype(bf16)

    @pl.loop(0, size // TILE)
    def _(t):
        subtract(lambda rows: flat[2, rows, at(t)], at(t))

        def store(i, x):
            second[i * TILE : (i + 1) * TILE, at(t)] = x.astype(bf16)

        lower(1, lambda n: updated[:n, at(t)], store)

    subtract(lambda rows: side[1, rows, :], slice(size, size + TILE))

    def store_side_two(i, x):
        second[i * TILE : (i + 1) * TILE, size:] = x.astype(bf16)

    lower(1, lambda n: updated[:n, size:], store_side_two)
    solved[1] = second[:, size + TILE // 2 :]

    rows = pl.ds(pl.multiple_of(own, 16), factor.shape[1])
    factor[0] = first[rows, :size]
    factor[1] = second[rows, :size]

    one = first[:, size:].T
    two = second[:, size:].T

    @pl.loop(0, size // TILE)
    def _(t):
        change = jnp.dot(one, first[:, at(t)], preferred_element_type=f32)
        change += jnp.dot(two, second[:, at(t)], preferred_element_type=f32)
        change = change.T
        trailing[at(t), :] = gram[at(t), :].astype(f32) - change[:, : TILE // 2]
        residual[at(t), :] = right[at(t), :].astype(f32) - change[:, TILE // 2 :]


def gather_small(block, axis, size):
    flat = block.reshape(1, -1, block.shape[-1])
    out = lax.all_to_all(jnp.tile(flat, (size, 1, 1)), axis, 0, 0, tiled=True)
    return out.reshape((size,) + block.shape)


def shift(block, axis, size, by):
    return lax.ppermute(block, axis, [(i, (i + by) % size) for i in range(size)])


def per_device(sizes, panel_top, panel_low, panel_next, gram_rest, inverses, right_top, right_low):
    rows, ys, cores, voxes = sizes
    axes = ("row", "y", "core", "vox")
    order = np.arange(rows * ys * cores * voxes).reshape(sizes)
    swap = list(zip(order.ravel().tolist(), order.transpose(1, 0, 2, 3).ravel().tolist()))
    z, y = lax.axis_index("row"), lax.axis_index("y")
    core, vox = lax.axis_index("core"), lax.axis_index("vox")
    size, width = inverses.shape[2], panel_low.shape[1]
    cols = gram_rest.shape[1]
    bf16 = jnp.bfloat16
    other = [(0, 1), (1, 0)]

    low, following = panel_low.T, panel_next.T
    pair = jnp.stack([low, following])
    swapped = lax.ppermute(pair, axes, swap)

    top = gather_small(panel_top.T, "row", rows).transpose(1, 0, 2).reshape(width, -1)
    panels = gather_small(jnp.stack([top, low, following]), "vox", voxes)
    panels, swapped = lax.optimization_barrier((panels, swapped))
    panel_own = lax.all_gather(panels, "y", axis=0)

    mine = lax.dynamic_index_in_dim(inverses, core, 0, False)
    blocks = swapped.reshape(2, width, cores * voxes, cols).transpose(2, 0, 1, 3)
    up, down = shift(mine, "row", rows, 1), shift(mine, "row", rows, -1)
    blocks = lax.all_to_all(blocks, ("core", "vox"), 0, 0, tiled=True)
    pieces = {0: mine, 1: up, rows - 1: down}
    for k in range(2, rows // 2 + 1):
        if k == 2:
            up, down, blocks = lax.optimization_barrier((up, down, blocks))
        if k == 3:
            up, down, matching = lax.optimization_barrier((up, down, matching))
        pieces[k] = up = shift(up, "row", rows, 1)
        if k < rows - k:
            pieces[rows - k] = down = shift(down, "row", rows, -1)
        if k == 2:
            matching = gather_small(blocks, "row", rows)
    inv_own = jnp.stack([pieces[k] for k in range(rows)])
    inv_other = lax.ppermute(inv_own, "core", other)
    matching = jnp.moveaxis(matching, 2, 0)
    matching = matching.reshape(2, size, cols)
    sides = [jnp.concatenate([matching[k], right_top[k]], axis=1) for k in range(2)]

    panel_own, inv_other, sides = lax.optimization_barrier((panel_own, inv_other, sides))
    panel_other = lax.ppermute(panel_own, "core", other)

    own = ((y * cores + core) * voxes + vox) * width
    where = jnp.stack([z, core, own]).astype(jnp.int32)
    height = panel_low.shape[0]
    any_space = pl.BlockSpec(memory_space=pl.ANY)
    local = pl.BlockSpec(memory_space=pltpu.VMEM)
    vmem = pltpu.VMEM
    flops = 2 * size * size * (2 * size + TILE + 2 * (size + TILE) + 2 * TILE)
    factor, solved, trailing, residual = pl.pallas_call(
        factor_kernel,
        out_shape=(
            jax.ShapeDtypeStruct((2, width, height), bf16),
            jax.ShapeDtypeStruct((2, size, cols), bf16),
            jax.ShapeDtypeStruct((height, cols), jnp.float32),
            jax.ShapeDtypeStruct((height, cols), jnp.float32),
        ),
        in_specs=[pl.BlockSpec(memory_space=pltpu.SMEM)] + [any_space] * 6 + [local] * 2,
        out_specs=(local,) * 4,
        scratch_shapes=[
            vmem((2, rows, size // rows, size), bf16),
            vmem((3, ys, cores, voxes, width, height), bf16),
            vmem((2, size, TILE), bf16),
            vmem((size, size), bf16),
            vmem((size, height + TILE), bf16),
            vmem((size, height + TILE), bf16),
            vmem((size, height + TILE), bf16),
            pltpu.SemaphoreType.DMA((2 * rows + 8,)),
        ],
        compiler_params=pltpu.CompilerParams(vmem_limit_bytes=48 * 1024 * 1024),
        cost_estimate=pl.CostEstimate(flops=flops, bytes_accessed=14 << 20, transcendentals=0),
        name="factor_and_update",
    )(where, inv_own, inv_other, panel_own, panel_other, sides[0], sides[1], gram_rest, right_low)
    return (factor.transpose(0, 2, 1), solved, trailing, residual)


def solution(mesh):
    cores = 2
    sizes = (mesh.shape["row"], mesh.shape["col"] // cores, cores, mesh.shape["vox"])
    split = Mesh(mesh.devices.reshape(sizes), ("row", "y", "core", "vox"))
    cols = ("y", "core", "vox")
    in_specs = (
        P("row", cols),
        P("row", cols),
        P("row", cols),
        P("row", cols),
        P(None, "row", None),
        P(None, None, cols),
        P("row", cols),
    )
    out_specs = (
        P(None, "row", cols),
        P(None, None, cols),
        P("row", cols),
        P("row", cols),
    )
    return jax.shard_map(
        functools.partial(per_device, sizes),
        mesh=split,
        in_specs=in_specs,
        out_specs=out_specs,
        check_vma=False,
    )
```

```python
import functools

import jax
import jax.numpy as jnp
import numpy as np
from jax import lax
from jax.experimental import pallas as pl
from jax.experimental.pallas import tpu as pltpu
from jax.sharding import Mesh
from jax.sharding import PartitionSpec as P

TILE = 256


def factor_kernel(ys, at_ref, whole, *refs):
    pieces, others, refs = refs[:ys], refs[ys : 2 * ys], refs[2 * ys :]
    side_one, side_two, gram, right, factor, solved, trailing, residual = refs[:8]
    inv, panels, side, minuend, top, first, updated, second, sems = refs[8:]
    y, core, own = at_ref[0], at_ref[1], at_ref[2]
    size = first.shape[0]
    f32, bf16 = jnp.float32, jnp.bfloat16

    inv_copies = [
        pltpu.make_async_copy(whole.at[0], inv.at[0], sems.at[0]),
        pltpu.make_async_copy(whole.at[1], inv.at[1], sems.at[1]),
    ]
    panel_copies = [[], [], []]
    for p in range(3):
        for k in range(ys):
            spot = lax.rem(y + (ys - k), ys)
            for ref, half in ((pieces[k], core), (others[k], 1 - core)):
                panel_copies[p].append(
                    pltpu.make_async_copy(
                        ref.at[:, p],
                        panels.at[p, spot, half],
                        sems.at[2 + 2 * ys * p + len(panel_copies[p])],
                    )
                )
    side_copies = [
        pltpu.make_async_copy(side_one, side.at[0], sems.at[2 + 6 * ys]),
        pltpu.make_async_copy(side_two, side.at[1], sems.at[3 + 6 * ys]),
    ]
    late_copies = [
        pltpu.make_async_copy(gram, minuend.at[0], sems.at[4 + 6 * ys]),
        pltpu.make_async_copy(right, minuend.at[1], sems.at[5 + 6 * ys]),
    ]
    for copy in inv_copies + panel_copies[0] + panel_copies[1] + side_copies + panel_copies[2] + late_copies:
        copy.start()
    for copy in inv_copies:
        copy.wait()

    def inverse(k, i):
        return inv[k, i * TILE : (i + 1) * TILE, : (i + 1) * TILE]

    def lower(k, load, store):
        for i in range(size // TILE):
            store(i, jnp.dot(inverse(k, i), load((i + 1) * TILE), preferred_element_type=f32))

    def at(t):
        return pl.ds(pl.multiple_of(t * TILE, TILE), TILE)

    flat = panels.reshape(3, size, size)

    for copy in panel_copies[0]:
        copy.wait()

    @pl.loop(0, size // TILE)
    def _(t):
        def store(i, x):
            top[at(t), i * TILE : (i + 1) * TILE] = x.astype(bf16).T

        lower(0, lambda n: flat[0, :n, at(t)], store)

    for copy in panel_copies[1] + side_copies:
        copy.wait()

    @pl.loop(0, size // TILE)
    def _(t):
        def store(i, x):
            first[i * TILE : (i + 1) * TILE, at(t)] = x.astype(bf16)

        lower(0, lambda n: flat[1, :n, at(t)], store)

    def store_side_one(i, x):
        first[i * TILE : (i + 1) * TILE, size:] = x.astype(bf16)

    lower(0, lambda n: side[0, :n, :], store_side_one)
    solved[0] = first[:, size + TILE // 2 :]

    for copy in panel_copies[2]:
        copy.wait()

    def subtract(load, cols):
        for i in range(size // TILE):
            rows = slice(i * TILE, (i + 1) * TILE)
            change = jnp.dot(top[rows, :], first[:, cols], preferred_element_type=f32)
            updated[rows, cols] = (load(rows).astype(f32) - change).astype(bf16)

    @pl.loop(0, size // TILE)
    def _(t):
        subtract(lambda rows: flat[2, rows, at(t)], at(t))

        def store(i, x):
            second[i * TILE : (i + 1) * TILE, at(t)] = x.astype(bf16)

        lower(1, lambda n: updated[:n, at(t)], store)

    subtract(lambda rows: side[1, rows, :], slice(size, size + TILE))

    def store_side_two(i, x):
        second[i * TILE : (i + 1) * TILE, size:] = x.astype(bf16)

    lower(1, lambda n: updated[:n, size:], store_side_two)
    solved[1] = second[:, size + TILE // 2 :]

    rows = pl.ds(pl.multiple_of(own, 16), factor.shape[1])
    factor[0] = first[rows, :size]
    factor[1] = second[rows, :size]

    for copy in late_copies:
        copy.wait()
    one = first[:, size:].T
    two = second[:, size:].T

    @pl.loop(0, size // TILE)
    def _(t):
        change = jnp.dot(one, first[:, at(t)], preferred_element_type=f32)
        change += jnp.dot(two, second[:, at(t)], preferred_element_type=f32)
        change = change.T
        trailing[at(t), :] = minuend[0, at(t), :].astype(f32) - change[:, : TILE // 2]
        residual[at(t), :] = minuend[1, at(t), :].astype(f32) - change[:, TILE // 2 :]


def gather_small(block, axis, size):
    flat = block.reshape(1, -1, block.shape[-1])
    out = lax.all_to_all(jnp.tile(flat, (size, 1, 1)), axis, 0, 0, tiled=True)
    return out.reshape((size,) + block.shape)


def shift(block, axis, size, by):
    return lax.ppermute(block, axis, [(i, (i + by) % size) for i in range(size)])


def per_device(sizes, panel_top, panel_low, panel_next, gram_rest, inverses, right_top, right_low):
    rows, ys, cores, voxes = sizes
    axes = ("row", "y", "core", "vox")
    order = np.arange(rows * ys * cores * voxes).reshape(sizes)
    swap = list(zip(order.ravel().tolist(), order.transpose(1, 0, 2, 3).ravel().tolist()))
    z, y = lax.axis_index("row"), lax.axis_index("y")
    core, vox = lax.axis_index("core"), lax.axis_index("vox")
    size, width = inverses.shape[2], panel_low.shape[1]
    cols = gram_rest.shape[1]
    bf16 = jnp.bfloat16
    other = [(0, 1), (1, 0)]

    whole = lax.all_gather(inverses, "row", axis=1, tiled=True)
    low, following = panel_low.T, panel_next.T
    pair = jnp.stack([low, following])
    swapped = lax.ppermute(pair, axes, swap)

    top = gather_small(panel_top.T, "row", rows).transpose(1, 0, 2).reshape(width, -1)
    top, swapped = lax.optimization_barrier((top, swapped))
    panels = gather_small(jnp.stack([top, low, following]), "vox", voxes)
    blocks = swapped.reshape(2, width, cores * voxes, cols).transpose(2, 0, 1, 3)

    up = down = panels
    pieces, others = {0: panels}, {}
    for k in range(1, ys // 2 + 1):
        if k == 2:
            up, down, blocks = lax.optimization_barrier((up, down, blocks))
        if k == 4:
            up, matching, whole = lax.optimization_barrier((up, matching, whole))
        if k == 1:
            blocks = lax.all_to_all(blocks, ("core", "vox"), 0, 0, tiled=True)
        if k == 2:
            matching = gather_small(blocks, "row", rows)
        pieces[k] = up = shift(up, "y", ys, 1)
        if k < ys - k:
            pieces[ys - k] = down = shift(down, "y", ys, -1)
    for k in range(ys):
        others[k] = lax.ppermute(pieces[k], "core", other)
    matching = jnp.moveaxis(matching, 2, 0)
    matching = matching.reshape(2, size, cols)
    sides = [jnp.concatenate([matching[k], right_top[k]], axis=1) for k in range(2)]
    pieces = [pieces[k] for k in range(ys)]
    others = [others[k] for k in range(ys)]

    own = ((y * cores + core) * voxes + vox) * width
    where = jnp.stack([y, core, own]).astype(jnp.int32)
    height = panel_low.shape[0]
    any_space = pl.BlockSpec(memory_space=pl.ANY)
    local = pl.BlockSpec(memory_space=pltpu.VMEM)
    vmem = pltpu.VMEM
    flops = 2 * size * size * (2 * size + TILE + 2 * (size + TILE) + 2 * TILE)
    factor, solved, trailing, residual = pl.pallas_call(
        functools.partial(factor_kernel, ys),
        out_shape=(
            jax.ShapeDtypeStruct((2, width, height), bf16),
            jax.ShapeDtypeStruct((2, size, cols), bf16),
            jax.ShapeDtypeStruct((height, cols), jnp.float32),
            jax.ShapeDtypeStruct((height, cols), jnp.float32),
        ),
        in_specs=[pl.BlockSpec(memory_space=pltpu.SMEM)] + [any_space] * (5 + 2 * ys),
        out_specs=(local,) * 4,
        scratch_shapes=[
            vmem((2, size, size), bf16),
            vmem((3, ys, cores, voxes, width, height), bf16),
            vmem((2, size, TILE), bf16),
            vmem((2, height, cols), bf16),
            vmem((size, size), bf16),
            vmem((size, height + TILE), bf16),
            vmem((size, height + TILE), bf16),
            vmem((size, height + TILE), bf16),
            pltpu.SemaphoreType.DMA((6 * ys + 6,)),
        ],
        compiler_params=pltpu.CompilerParams(vmem_limit_bytes=40 * 1024 * 1024),
        cost_estimate=pl.CostEstimate(flops=flops, bytes_accessed=14 << 20, transcendentals=0),
        name="factor_and_update",
    )(where, whole, *pieces, *others, *sides, gram_rest, right_low)
    return (factor.transpose(0, 2, 1), solved, trailing, residual)


def solution(mesh):
    cores = 2
    sizes = (mesh.shape["row"], mesh.shape["col"] // cores, cores, mesh.shape["vox"])
    split = Mesh(mesh.devices.reshape(sizes), ("row", "y", "core", "vox"))
    cols = ("y", "core", "vox")
    in_specs = (
        P("row", cols),
        P("row", cols),
        P("row", cols),
        P("row", cols),
        P(None, "row", None),
        P(None, None, cols),
        P("row", cols),
    )
    out_specs = (
        P(None, "row", cols),
        P(None, None, cols),
        P("row", cols),
        P("row", cols),
    )
    return jax.shard_map(
        functools.partial(per_device, sizes),
        mesh=split,
        in_specs=in_specs,
        out_specs=out_specs,
        check_vma=False,
    )
```

```python
import functools

import jax
import jax.numpy as jnp
import numpy as np
from jax import lax
from jax.experimental import pallas as pl
from jax.experimental.pallas import tpu as pltpu
from jax.sharding import Mesh
from jax.sharding import PartitionSpec as P

TILE = 256
F32, BF16 = jnp.float32, jnp.bfloat16


def lower(inv, load, store):
    for i in range(inv.shape[0] // TILE):
        n = (i + 1) * TILE
        left = inv[i * TILE : n, :n]
        store(i, jnp.dot(left, load(n), preferred_element_type=F32))


def piece(t):
    return slice(t * TILE, (t + 1) * TILE)


def start_copies(pairs, sems, base=0):
    copies = [
        pltpu.make_async_copy(src, dst, sems.at[base + i]) for i, (src, dst) in enumerate(pairs)
    ]
    for copy in copies:
        copy.start()
    return copies


def wait(copies):
    for copy in copies:
        copy.wait()


def ordered(pieces, p, y, panel):
    count = len(pieces)
    return [(pieces[k].at[p], panel.at[:, lax.rem(y + (count - k), count)]) for k in range(count)]


def flatten(panel):
    return panel.reshape(panel.shape[0], -1, panel.shape[-1])


def pack_kernel(low, following, sent):
    cores, voxes = sent.shape[:2]
    cols = sent.shape[-1]
    for p, ref in enumerate((low, following)):
        for core in range(cores):
            for vox in range(voxes):
                for j in range(voxes + 1):
                    at = (core * voxes + (vox if j == voxes else j)) * cols
                    sent[core, vox, j, p] = ref[:, at : at + cols]


def unpack_kernel(got, mine, single):
    group, slots = got.shape[:2]
    for src in range(group):
        single[src] = got[src, slots - 1]
        for p in range(2):
            for j in range(slots - 1):
                mine[p, j, src] = got[src, j, p]


def top_kernel(whole, blocks, top, inv, panel, result, sems):
    loads = [(whole.at[0], inv)]
    loads += [(blocks.at[:, y], panel.at[y]) for y in range(panel.shape[0])]
    wait(start_copies(loads, sems))
    flat = panel.reshape(-1, panel.shape[-1])
    stores = []
    for t in range(top.shape[0] // TILE):

        def store(i, x):
            result[piece(t), piece(i)] = x.astype(BF16).T

        lower(inv, lambda n: flat[:n, piece(t)], store)
        stores += start_copies([(result.at[piece(t)], top.at[piece(t)])], sems, t)
    wait(stores)


def first_kernel(ys, at_ref, whole, *refs):
    pieces, (first, inv, panel, result, sems) = refs[:ys], refs[ys:]
    loads = [(whole.at[0], inv)] + ordered(pieces, 0, at_ref[0], panel)
    wait(start_copies(loads, sems))
    flat = flatten(panel)
    for t in range(first.shape[1] // TILE):

        def load(n):
            return jnp.concatenate([flat[2 * t, :n], flat[2 * t + 1, :n]], axis=1)

        def store(i, x):
            result[piece(i), piece(t)] = x.astype(BF16)

        lower(inv, load, store)
    wait(start_copies([(result, first)], sems))


def second_kernel(ys, at_ref, whole, top_own, top_other, first, *refs):
    pieces, refs = refs[:ys], refs[ys:]
    second, inv, panel, top, left, updated, result, sems = refs
    core = at_ref[1]
    loads = [(top_own, top.at[0]), (first, left)] + ordered(pieces, 1, at_ref[0], panel)
    early = start_copies(loads, sems)
    late = start_copies([(top_other, top.at[1]), (whole.at[1], inv)], sems, len(loads))
    wait(early)
    flat = flatten(panel)
    half = top_own.shape[0]
    for part, side in ((0, core), (1, 1 - core)):
        if part == 1:
            wait(late)
        for t in range(first.shape[1] // TILE):
            for i in range(half // TILE):
                rows = pl.ds(pl.multiple_of(side * half + i * TILE, TILE), TILE)
                change = jnp.dot(
                    top[part, piece(i)], left[:, piece(t)], preferred_element_type=F32
                )
                old = jnp.concatenate([flat[2 * t, rows], flat[2 * t + 1, rows]], axis=1)
                updated[rows, piece(t)] = (old.astype(F32) - change).astype(BF16)
    for t in range(first.shape[1] // TILE):

        def store(i, x):
            result[piece(i), piece(t)] = x.astype(BF16)

        lower(inv, lambda n: updated[:n, piece(t)], store)
    wait(start_copies([(result, second)], sems))


def side_kernel(
    at_ref, whole, top_own, top_other, side_one, side_two, first, second, inv, top, updated, sems
):
    core = at_ref[1]
    half = top_own.shape[0]
    early = start_copies([(whole.at[0], inv.at[0])], sems)
    late = start_copies(
        [(top_own, top.at[0]), (top_other, top.at[1]), (whole.at[1], inv.at[1])], sems, 1
    )
    wait(early)

    def store_first(i, x):
        first[piece(i), :] = x.astype(BF16)

    lower(inv.at[0], lambda n: side_one[:n, :], store_first)
    wait(late)
    for part, side in ((0, core), (1, 1 - core)):
        for i in range(half // TILE):
            rows = pl.ds(pl.multiple_of(side * half + i * TILE, TILE), TILE)
            change = jnp.dot(top[part, piece(i)], first[...], preferred_element_type=F32)
            updated[rows, :] = (side_two[rows, :].astype(F32) - change).astype(BF16)

    def store_second(i, x):
        second[piece(i), :] = x.astype(BF16)

    lower(inv.at[1], lambda n: updated[:n, :], store_second)


def rest_kernel(
    at_ref, first_own, first_other, second_own, second_other, side_one, side_two, gram, right,
    factor, solved, trailing, residual, first, second, minuend, sems,
):
    core, own = at_ref[1], at_ref[2]
    half = first_own.shape[1]
    cols = gram.shape[1]
    loads = [
        start_copies([(first_own, first.at[0]), (second_own, second.at[0])], sems),
        start_copies([(first_other, first.at[1]), (second_other, second.at[1])], sems, 2),
    ]
    loads[0] += start_copies([(gram, minuend.at[0]), (right, minuend.at[1])], sems, 4)
    solved[0] = side_one[:, cols:]
    solved[1] = side_two[:, cols:]
    one, two = side_one[...].T, side_two[...].T
    mine = pl.ds(pl.multiple_of(own, 16), factor.shape[1])
    for part, side in ((0, core), (1, 1 - core)):
        wait(loads[part])
        base = pl.multiple_of(side * half, half)
        factor[0, :, pl.ds(base, half)] = first[part, mine, :]
        factor[1, :, pl.ds(base, half)] = second[part, mine, :]
        for t in range(half // TILE):
            change = jnp.dot(one, first[part, :, piece(t)], preferred_element_type=F32)
            change += jnp.dot(two, second[part, :, piece(t)], preferred_element_type=F32)
            change = change.T
            rows = pl.ds(pl.multiple_of(base + t * TILE, TILE), TILE)
            trailing[rows, :] = minuend[0, rows, :].astype(F32) - change[:, :cols]
            residual[rows, :] = minuend[1, rows, :].astype(F32) - change[:, cols:]


def exchange(blocks, axis):
    flat = blocks.reshape(blocks.shape[0], -1, blocks.shape[-1])
    return lax.all_to_all(flat, axis, 0, 0, tiled=True).reshape(blocks.shape)


def gather_small(block, axis, size):
    return exchange(jnp.broadcast_to(block[None], (size,) + block.shape), axis)


def shift(block, axis, size, by):
    return lax.ppermute(block, axis, [(i, (i + by) % size) for i in range(size)])


def call(body, name, outs, scratch, flops, *operands, small=False):
    local = pl.BlockSpec(memory_space=pltpu.VMEM)
    anywhere = pl.BlockSpec(memory_space=pl.ANY)
    specs = [
        pl.BlockSpec(memory_space=pltpu.SMEM) if x.dtype == jnp.int32
        else local if small or x.shape[-1] == TILE else anywhere
        for x in operands
    ]
    moved = sum(x.size * x.dtype.itemsize for x in operands)
    return pl.pallas_call(
        body,
        name=name,
        out_shape=tuple(jax.ShapeDtypeStruct(shape, dtype) for shape, dtype in outs),
        in_specs=specs,
        out_specs=(local if small or len(outs) > 1 else anywhere,) * len(outs),
        scratch_shapes=scratch,
        compiler_params=pltpu.CompilerParams(vmem_limit_bytes=(8 if small else 56) << 20),
        cost_estimate=pl.CostEstimate(flops=flops, bytes_accessed=moved, transcendentals=0),
    )(*operands)


def per_device(sizes, panel_top, panel_low, panel_next, gram_rest, inverses, right_top, right_low):
    rows, ys, cores, voxes = sizes
    axes = ("row", "y", "core", "vox")
    near = ("core", "vox")
    order = np.arange(rows * ys * cores * voxes).reshape(sizes)
    swap = list(zip(order.ravel().tolist(), order.transpose(1, 0, 2, 3).ravel().tolist()))
    y, core, vox = lax.axis_index("y"), lax.axis_index("core"), lax.axis_index("vox")
    size, (height, width) = inverses.shape[2], panel_low.shape
    cols = gram_rest.shape[1]
    half = height // cores
    group = cores * voxes
    other = [(0, 1), (1, 0)]

    whole = lax.all_gather(inverses, "row", axis=1, tiled=True)

    (sent,) = call(
        pack_kernel, "pack", [((cores, voxes, voxes + 1, 2, width, cols), BF16)], [], 0,
        panel_low.T, panel_next.T, small=True,
    )
    got = exchange(sent.reshape((group,) + sent.shape[2:]), near)
    mine, single = call(
        unpack_kernel, "unpack",
        [((2, voxes, group, width, cols), BF16), ((group, 2, width, cols), BF16)], [], 0,
        got, small=True,
    )
    mine = mine.reshape(2, voxes, group * width, cols)
    swapped = lax.ppermute(single, axes, swap)

    def ring(k):
        up = shift(pieces[k - 1], "y", ys, 1)
        down = shift(pieces[(ys - k + 1) % ys], "y", ys, -1) if k < ys - k else None
        return up, down

    pieces = {0: mine}
    top, pieces[0] = lax.optimization_barrier((panel_top.T, pieces[0]))
    pieces[1], pieces[ys - 1] = ring(1)
    top = gather_small(top, "row", rows).transpose(1, 0, 2).reshape(width, size)
    top, pieces[1], pieces[ys - 1] = lax.optimization_barrier((top, pieces[1], pieces[ys - 1]))
    pieces[2], pieces[ys - 2] = ring(2)
    tops = gather_small(top, "y", ys)
    tops, pieces[2], pieces[ys - 2] = lax.optimization_barrier((tops, pieces[2], pieces[ys - 2]))
    pieces[3], pieces[ys - 3] = ring(3)
    blocks = tops.reshape(ys, width, cores, size // cores).transpose(2, 0, 1, 3)
    blocks = jnp.broadcast_to(blocks[:, None], (cores, voxes) + blocks.shape[1:])
    blocks = exchange(blocks.reshape((group,) + blocks.shape[2:]), near)
    blocks, swapped, pieces[3], pieces[ys - 3] = lax.optimization_barrier(
        (blocks, swapped, pieces[3], pieces[ys - 3])
    )
    pieces[4], _ = ring(4)
    matching = gather_small(swapped, "row", rows)
    matching = jnp.moveaxis(matching, 2, 0).reshape(2, size, cols)
    pieces = [pieces[k] for k in range(ys)]

    own = ((y * cores + core) * voxes + vox) * width
    where = jnp.stack([y, core, own]).astype(jnp.int32)
    sems = pltpu.SemaphoreType.DMA((ys + 4,))
    panel = pltpu.VMEM((voxes, ys, group * width, cols), BF16)
    square = pltpu.VMEM((size, size), BF16)
    tall = pltpu.VMEM((size, half), BF16)
    work = 2 * size * size

    (top_own,) = call(
        top_kernel, "top", [((size // cores, size), BF16)],
        [square, pltpu.VMEM((ys, group, width, size // cores), BF16),
         pltpu.VMEM((size // cores, size), BF16), sems],
        work * size // cores, whole, blocks,
    )
    top_other = lax.ppermute(top_own, "core", other)
    (first_own,) = call(
        functools.partial(first_kernel, ys), "first", [((size, half), BF16)],
        [square, panel, tall, sems], work * half, where, whole, *pieces,
    )
    first_other = lax.ppermute(first_own, "core", other)
    (second_own,) = call(
        functools.partial(second_kernel, ys), "second", [((size, half), BF16)],
        [square, panel, pltpu.VMEM((cores, size // cores, size), BF16), tall, tall, tall, sems],
        2 * work * half, where, whole, top_own, top_other, first_own, *pieces,
    )
    second_other = lax.ppermute(second_own, "core", other)
    sides = [jnp.concatenate([matching[k], right_top[k]], axis=1) for k in range(2)]
    side_one, side_two = call(
        side_kernel, "side", [((size, 2 * cols), BF16)] * 2,
        [pltpu.VMEM((2, size, size), BF16), pltpu.VMEM((cores, size // cores, size), BF16),
         pltpu.VMEM((size, 2 * cols), BF16), sems],
        6 * work * cols, where, whole, top_own, top_other, *sides,
    )
    factor, solved, trailing, residual = call(
        rest_kernel, "rest",
        [((2, width, height), BF16), ((2, size, cols), BF16)] + [((height, cols), F32)] * 2,
        [pltpu.VMEM((cores, size, half), BF16)] * 2 + [pltpu.VMEM((2, height, cols), BF16), sems],
        4 * work * cols, where, first_own, first_other, second_own, second_other,
        side_one, side_two, gram_rest, right_low,
    )
    return (factor.transpose(0, 2, 1), solved, trailing, residual)


def solution(mesh):
    cores = 2
    sizes = (mesh.shape["row"], mesh.shape["col"] // cores, cores, mesh.shape["vox"])
    split = Mesh(mesh.devices.reshape(sizes), ("row", "y", "core", "vox"))
    cols = ("y", "core", "vox")
    in_specs = (
        P("row", cols),
        P("row", cols),
        P("row", cols),
        P("row", cols),
        P(None, "row", None),
        P(None, None, cols),
        P("row", cols),
    )
    out_specs = (
        P(None, "row", cols),
        P(None, None, cols),
        P("row", cols),
        P("row", cols),
    )
    return jax.shard_map(
        functools.partial(per_device, sizes),
        mesh=split,
        in_specs=in_specs,
        out_specs=out_specs,
        check_vma=False,
    )
```

```python
import functools

import jax
import jax.numpy as jnp
import numpy as np
from jax import lax
from jax.experimental import pallas as pl
from jax.experimental.pallas import tpu as pltpu
from jax.sharding import Mesh
from jax.sharding import PartitionSpec as P

TILE = 256


def start_copies(pairs, sems):
    copies = [pltpu.make_async_copy(src, dst, sems.at[i]) for i, (src, dst) in enumerate(pairs)]
    for copy in copies:
        copy.start()
    return copies


def wait(copies):
    for copy in copies:
        copy.wait()


def pack_kernel(top, low, following, sent):
    cores, voxes = sent.shape[:2]
    cols = sent.shape[-1]
    for core in range(cores):
        for vox in range(voxes):
            for j in range(voxes):
                chunk = core * voxes + j
                at = slice(chunk * cols, (chunk + 1) * cols)
                sent[core, vox, j] = top[chunk]
                sent[core, vox, voxes + j] = low[:, at]
                sent[core, vox, 2 * voxes + j] = following[:, at]
            chunk = core * voxes + vox
            at = slice(chunk * cols, (chunk + 1) * cols)
            sent[core, vox, 3 * voxes] = low[:, at]
            sent[core, vox, 3 * voxes + 1] = following[:, at]


def unpack_kernel(got, mine, single):
    group, slots = got.shape[:2]
    for src in range(group):
        for j in range(slots - 2):
            mine[j, src] = got[src, j]
        single[src, 0] = got[src, slots - 2]
        single[src, 1] = got[src, slots - 1]


def stack_kernel(*refs):
    pieces, stacked, sems = refs[:-2], refs[-2], refs[-1]
    wait(start_copies([(ref, stacked.at[i]) for i, ref in enumerate(pieces)], sems))


def order_kernel(at_ref, *refs):
    pieces, stacked, sems = refs[:-2], refs[-2], refs[-1]
    n = len(pieces)
    wait(
        start_copies(
            [(ref, stacked.at[lax.rem(at_ref[3] + (n - k), n)]) for k, ref in enumerate(pieces)],
            sems,
        )
    )


def factor_kernel(near, ys, at_ref, inv_own, inv_other, *refs):
    pieces, refs = refs[:ys], refs[ys:]
    far_near, far_rest, refs = refs[0], refs[1], refs[2:]
    others = {k: (far_near, i) for i, k in enumerate(near)}
    others |= {k: (far_rest, i) for i, k in enumerate(k for k in range(ys) if k not in near)}
    side_one, side_two, gram, right, factor, solved, trailing, residual = refs[:8]
    inv, panels, side, minuend, top, first, updated, second, sems = refs[8:]
    y, core, own = at_ref[0], at_ref[1], at_ref[2]
    size = first.shape[0]
    voxes = panels.shape[1] // 2
    f32, bf16 = jnp.float32, jnp.bfloat16

    inv_copies = [
        pltpu.make_async_copy(inv_own, inv.at[core], sems.at[0]),
        pltpu.make_async_copy(inv_other, inv.at[1 - core], sems.at[1]),
    ]
    panel_copies = [[], [], []]
    for p in range(3):
        part = slice(p * voxes, (p + 1) * voxes)
        for k in range(ys):
            spot = lax.rem(y + (ys - k), ys)
            far, i = others[k]
            for ref, half in ((pieces[k].at[part], core), (far.at[i, part], 1 - core)):
                panel_copies[p].append(
                    pltpu.make_async_copy(
                        ref,
                        panels.at[p, pl.ds(half * voxes, voxes), spot],
                        sems.at[2 + 2 * ys * p + len(panel_copies[p])],
                    )
                )
    side_copies = [
        pltpu.make_async_copy(side_one, side.at[0], sems.at[2 + 6 * ys]),
        pltpu.make_async_copy(side_two, side.at[1], sems.at[3 + 6 * ys]),
    ]
    late_copies = [
        pltpu.make_async_copy(gram, minuend.at[0], sems.at[4 + 6 * ys]),
        pltpu.make_async_copy(right, minuend.at[1], sems.at[5 + 6 * ys]),
    ]
    for copy in inv_copies + panel_copies[0] + panel_copies[1] + side_copies + panel_copies[2] + late_copies:
        copy.start()
    for copy in inv_copies:
        copy.wait()

    def inverse(k, i):
        rows = inv[k, 2 * i : 2 * i + 2].reshape(TILE, size)
        return rows[:, : (i + 1) * TILE]

    def lower(k, load, store):
        for i in range(size // TILE):
            store(i, jnp.dot(inverse(k, i), load((i + 1) * TILE), preferred_element_type=f32))

    def at(t):
        return pl.ds(pl.multiple_of(t * TILE, TILE), TILE)

    flat = panels.reshape(panels.shape[:2] + (size, panels.shape[-1]))

    def tile(p, rows, t):
        return jnp.concatenate([flat[p, 2 * t, rows], flat[p, 2 * t + 1, rows]], axis=1)

    for copy in panel_copies[0]:
        copy.wait()

    @pl.loop(0, size // TILE)
    def _(t):
        def store(i, x):
            top[at(t), i * TILE : (i + 1) * TILE] = x.astype(bf16).T

        lower(0, lambda n: tile(0, slice(n), t), store)

    for copy in panel_copies[1] + side_copies:
        copy.wait()

    @pl.loop(0, size // TILE)
    def _(t):
        def store(i, x):
            first[i * TILE : (i + 1) * TILE, at(t)] = x.astype(bf16)

        lower(0, lambda n: tile(1, slice(n), t), store)

    def store_side_one(i, x):
        first[i * TILE : (i + 1) * TILE, size:] = x.astype(bf16)

    lower(0, lambda n: side[0, :n, :], store_side_one)
    solved[0] = first[:, size + TILE // 2 :]

    for copy in panel_copies[2]:
        copy.wait()

    def subtract(load, cols):
        for i in range(size // TILE):
            rows = slice(i * TILE, (i + 1) * TILE)
            change = jnp.dot(top[rows, :], first[:, cols], preferred_element_type=f32)
            updated[rows, cols] = (load(rows).astype(f32) - change).astype(bf16)

    @pl.loop(0, size // TILE)
    def _(t):
        subtract(lambda rows: tile(2, rows, t), at(t))

        def store(i, x):
            second[i * TILE : (i + 1) * TILE, at(t)] = x.astype(bf16)

        lower(1, lambda n: updated[:n, at(t)], store)

    subtract(lambda rows: side[1, rows, :], slice(size, size + TILE))

    def store_side_two(i, x):
        second[i * TILE : (i + 1) * TILE, size:] = x.astype(bf16)

    lower(1, lambda n: updated[:n, size:], store_side_two)
    solved[1] = second[:, size + TILE // 2 :]

    rows = pl.ds(pl.multiple_of(own, 16), factor.shape[1])
    factor[0] = first[rows, :size]
    factor[1] = second[rows, :size]

    for copy in late_copies:
        copy.wait()
    one = first[:, size:].T
    two = second[:, size:].T

    @pl.loop(0, size // TILE)
    def _(t):
        change = jnp.dot(one, first[:, at(t)], preferred_element_type=f32)
        change += jnp.dot(two, second[:, at(t)], preferred_element_type=f32)
        change = change.T
        trailing[at(t), :] = minuend[0, at(t), :].astype(f32) - change[:, : TILE // 2]
        residual[at(t), :] = minuend[1, at(t), :].astype(f32) - change[:, TILE // 2 :]


def exchange(blocks, axis):
    flat = blocks.reshape(blocks.shape[0], -1, blocks.shape[-1])
    return lax.all_to_all(flat, axis, 0, 0, tiled=True).reshape(blocks.shape)


def gather_small(block, axis, size):
    return exchange(jnp.broadcast_to(block[None], (size,) + block.shape), axis)


def shift(block, axis, size, by):
    return lax.ppermute(block, axis, [(i, (i + by) % size) for i in range(size)])


def call(body, name, outs, *operands):
    local = pl.BlockSpec(memory_space=pltpu.VMEM)
    return pl.pallas_call(
        body,
        name=name,
        out_shape=tuple(jax.ShapeDtypeStruct(shape, dtype) for shape, dtype in outs),
        in_specs=[local] * len(operands),
        out_specs=(local,) * len(outs),
        compiler_params=pltpu.CompilerParams(vmem_limit_bytes=2 << 20),
    )(*operands)


def stack(pieces, where=None):
    anywhere = pl.BlockSpec(memory_space=pl.ANY)
    extra = [] if where is None else [where]
    return pl.pallas_call(
        stack_kernel if where is None else order_kernel,
        name="stack" if where is None else "order",
        out_shape=jax.ShapeDtypeStruct((len(pieces),) + pieces[0].shape, pieces[0].dtype),
        in_specs=[pl.BlockSpec(memory_space=pltpu.SMEM)] * len(extra) + [anywhere] * len(pieces),
        out_specs=anywhere,
        scratch_shapes=[pltpu.SemaphoreType.DMA((len(pieces),))],
        compiler_params=pltpu.CompilerParams(vmem_limit_bytes=1 << 20),
    )(*extra, *pieces)


def per_device(sizes, panel_top, panel_low, panel_next, gram_rest, inverses, right_top, right_low):
    rows, ys, cores, voxes = sizes
    axes = ("row", "y", "core", "vox")
    order = np.arange(rows * ys * cores * voxes).reshape(sizes)
    swap = list(zip(order.ravel().tolist(), order.transpose(1, 0, 2, 3).ravel().tolist()))
    z, y = lax.axis_index("row"), lax.axis_index("y")
    core, vox = lax.axis_index("core"), lax.axis_index("vox")
    size, width = inverses.shape[2], panel_low.shape[1]
    cols = gram_rest.shape[1]
    bf16 = jnp.bfloat16
    other = [(0, 1), (1, 0)]

    own = ((y * cores + core) * voxes + vox) * width
    where = jnp.stack([y, core, own, z]).astype(jnp.int32)
    barrier = lax.optimization_barrier
    group = cores * voxes
    flats = [panel_low.T, panel_next.T]

    def ring(pieces, k, axis, n):
        up = pieces[k] = shift(pieces[k - 1], axis, n, 1)
        if k == n - k:
            return [up]
        down = pieces[n - k] = shift(pieces[(n - k + 1) % n], axis, n, -1)
        return [up, down]

    def ordered(values, pieces, k, n):
        keys = sorted({k, n - k})
        values, held = barrier((values, [pieces[i] for i in keys]))
        for i, piece in zip(keys, held):
            pieces[i] = piece
        return values

    invs = {0: lax.dynamic_index_in_dim(inverses, core, 0, False)}
    ring(invs, 1, "row", rows)
    top = gather_small(panel_top.T, "row", rows)
    top = ordered(top, invs, 1, rows)
    ring(invs, 2, "row", rows)
    (sent,) = call(
        pack_kernel, "pack", [((cores, voxes, 3 * voxes + 2, width, cols), bf16)], top, *flats
    )
    got = exchange(sent.reshape((group,) + sent.shape[2:]), ("core", "vox"))
    mine, single = call(
        unpack_kernel, "unpack",
        [((3 * voxes, group, width, cols), bf16), ((group, 2, width, cols), bf16)], got,
    )
    pieces = {0: mine.reshape(3 * voxes, group * width, cols)}
    pieces[0], single = ordered((pieces[0], single), invs, 2, rows)
    ring(pieces, 1, "y", ys)
    swapped = lax.ppermute(single, axes, swap)
    ring(invs, 3, "row", rows)
    swapped = ordered(ordered(swapped, invs, 3, rows), pieces, 1, ys)
    ring(pieces, 2, "y", ys)
    ring(invs, 4, "row", rows)
    matching = gather_small(swapped, "row", rows)
    invs[4] = ordered(invs[4], pieces, 2, ys)
    ring(pieces, 3, "y", ys)
    near = sorted(k % ys for k in range(-2, 3))
    far_near = lax.ppermute(stack([pieces[k] for k in near]), "core", other)
    inv_own = stack([invs[k] for k in range(rows)], where)
    inv_own, matching = ordered((inv_own, matching), pieces, 3, ys)
    inv_other = lax.ppermute(inv_own, "core", other)
    ring(pieces, 4, "y", ys)
    rest = [pieces[k] for k in range(ys) if k not in near]
    far_rest = lax.ppermute(stack(rest), "core", other)

    matching = jnp.moveaxis(matching, 2, 0).reshape(2, size, cols)
    sides = [jnp.concatenate([matching[k], right_top[k]], axis=1) for k in range(2)]
    pieces = [pieces[k] for k in range(ys)]

    height = panel_low.shape[0]
    any_space = pl.BlockSpec(memory_space=pl.ANY)
    local = pl.BlockSpec(memory_space=pltpu.VMEM)
    vmem = pltpu.VMEM
    flops = 2 * size * size * (2 * size + TILE + 2 * (size + TILE) + 2 * TILE)
    factor, solved, trailing, residual = pl.pallas_call(
        functools.partial(factor_kernel, near, ys),
        out_shape=(
            jax.ShapeDtypeStruct((2, width, height), bf16),
            jax.ShapeDtypeStruct((2, size, cols), bf16),
            jax.ShapeDtypeStruct((height, cols), jnp.float32),
            jax.ShapeDtypeStruct((height, cols), jnp.float32),
        ),
        in_specs=[pl.BlockSpec(memory_space=pltpu.SMEM)] + [any_space] * (8 + ys),
        out_specs=(local,) * 4,
        scratch_shapes=[
            vmem((2, rows, size // rows, size), bf16),
            vmem((3, cores * voxes, ys, group * width, cols), bf16),
            vmem((2, size, TILE), bf16),
            vmem((2, height, cols), bf16),
            vmem((size, size), bf16),
            vmem((size, height + TILE), bf16),
            vmem((size, height + TILE), bf16),
            vmem((size, height + TILE), bf16),
            pltpu.SemaphoreType.DMA((6 * ys + 6,)),
        ],
        compiler_params=pltpu.CompilerParams(vmem_limit_bytes=40 * 1024 * 1024),
        cost_estimate=pl.CostEstimate(flops=flops, bytes_accessed=14 << 20, transcendentals=0),
        name="factor_and_update",
    )(where, inv_own, inv_other, *pieces, far_near, far_rest, *sides, gram_rest, right_low)
    return (factor.transpose(0, 2, 1), solved, trailing, residual)


def solution(mesh):
    cores = 2
    sizes = (mesh.shape["row"], mesh.shape["col"] // cores, cores, mesh.shape["vox"])
    split = Mesh(mesh.devices.reshape(sizes), ("row", "y", "core", "vox"))
    cols = ("y", "core", "vox")
    in_specs = (
        P("row", cols),
        P("row", cols),
        P("row", cols),
        P("row", cols),
        P(None, "row", None),
        P(None, None, cols),
        P("row", cols),
    )
    out_specs = (
        P(None, "row", cols),
        P(None, None, cols),
        P("row", cols),
        P("row", cols),
    )
    return jax.shard_map(
        functools.partial(per_device, sizes),
        mesh=split,
        in_specs=in_specs,
        out_specs=out_specs,
        check_vma=False,
    )
```

```python
import functools

import jax
import jax.numpy as jnp
import numpy as np
from jax import lax
from jax.experimental import pallas as pl
from jax.experimental.pallas import tpu as pltpu
from jax.sharding import Mesh
from jax.sharding import PartitionSpec as P

TILE = 256


def start_copies(pairs, sems):
    copies = [pltpu.make_async_copy(src, dst, sems.at[i]) for i, (src, dst) in enumerate(pairs)]
    for copy in copies:
        copy.start()
    return copies


def wait(copies):
    for copy in copies:
        copy.wait()


def pack_kernel(top, low, following, sent):
    cores, voxes = sent.shape[:2]
    cols = sent.shape[-1]
    for core in range(cores):
        for vox in range(voxes):
            for j in range(voxes):
                chunk = core * voxes + j
                at = slice(chunk * cols, (chunk + 1) * cols)
                sent[core, vox, j] = top[chunk]
                sent[core, vox, voxes + j] = low[:, at]
                sent[core, vox, 2 * voxes + j] = following[:, at]
            chunk = core * voxes + vox
            at = slice(chunk * cols, (chunk + 1) * cols)
            sent[core, vox, 3 * voxes] = low[:, at]
            sent[core, vox, 3 * voxes + 1] = following[:, at]


def unpack_kernel(got, mine, single):
    group, slots = got.shape[:2]
    for src in range(group):
        for j in range(slots - 2):
            mine[j, src] = got[src, j]
        single[src, 0] = got[src, slots - 2]
        single[src, 1] = got[src, slots - 1]


def stack_kernel(*refs):
    pieces, stacked, sems = refs[:-2], refs[-2], refs[-1]
    wait(start_copies([(ref, stacked.at[i]) for i, ref in enumerate(pieces)], sems))


def factor_kernel(near, ys, at_ref, whole, *refs):
    pieces, refs = refs[:ys], refs[ys:]
    far_near, far_rest, refs = refs[0], refs[1], refs[2:]
    others = {k: (far_near, i) for i, k in enumerate(near)}
    others |= {k: (far_rest, i) for i, k in enumerate(k for k in range(ys) if k not in near)}
    side_one, side_two, gram, right, factor, solved, trailing, residual = refs[:8]
    inv, panels, side, minuend, top, first, updated, second, sems = refs[8:]
    y, core, own = at_ref[0], at_ref[1], at_ref[2]
    size = first.shape[0]
    voxes = panels.shape[1] // 2
    f32, bf16 = jnp.float32, jnp.bfloat16

    inv_copies = [
        pltpu.make_async_copy(whole.at[0], inv.at[0], sems.at[0]),
        pltpu.make_async_copy(whole.at[1], inv.at[1], sems.at[1]),
    ]
    panel_copies = [[], [], []]
    for p in range(3):
        part = slice(p * voxes, (p + 1) * voxes)
        for k in range(ys):
            spot = lax.rem(y + (ys - k), ys)
            far, i = others[k]
            for ref, half in ((pieces[k].at[part], core), (far.at[i, part], 1 - core)):
                panel_copies[p].append(
                    pltpu.make_async_copy(
                        ref,
                        panels.at[p, pl.ds(half * voxes, voxes), spot],
                        sems.at[2 + 2 * ys * p + len(panel_copies[p])],
                    )
                )
    side_copies = [
        pltpu.make_async_copy(side_one, side.at[0], sems.at[2 + 6 * ys]),
        pltpu.make_async_copy(side_two, side.at[1], sems.at[3 + 6 * ys]),
    ]
    late_copies = [
        pltpu.make_async_copy(gram, minuend.at[0], sems.at[4 + 6 * ys]),
        pltpu.make_async_copy(right, minuend.at[1], sems.at[5 + 6 * ys]),
    ]
    for copy in inv_copies + panel_copies[0] + panel_copies[1] + side_copies + panel_copies[2] + late_copies:
        copy.start()
    for copy in inv_copies:
        copy.wait()

    def inverse(k, i):
        return inv[k, i * TILE : (i + 1) * TILE, : (i + 1) * TILE]

    def lower(k, load, store):
        for i in range(size // TILE):
            store(i, jnp.dot(inverse(k, i), load((i + 1) * TILE), preferred_element_type=f32))

    def at(t):
        return pl.ds(pl.multiple_of(t * TILE, TILE), TILE)

    flat = panels.reshape(panels.shape[:2] + (size, panels.shape[-1]))

    def tile(p, rows, t):
        return jnp.concatenate([flat[p, 2 * t, rows], flat[p, 2 * t + 1, rows]], axis=1)

    for copy in panel_copies[0]:
        copy.wait()

    @pl.loop(0, size // TILE)
    def _(t):
        def store(i, x):
            top[at(t), i * TILE : (i + 1) * TILE] = x.astype(bf16).T

        lower(0, lambda n: tile(0, slice(n), t), store)

    for copy in panel_copies[1] + side_copies:
        copy.wait()

    @pl.loop(0, size // TILE)
    def _(t):
        def store(i, x):
            first[i * TILE : (i + 1) * TILE, at(t)] = x.astype(bf16)

        lower(0, lambda n: tile(1, slice(n), t), store)

    def store_side_one(i, x):
        first[i * TILE : (i + 1) * TILE, size:] = x.astype(bf16)

    lower(0, lambda n: side[0, :n, :], store_side_one)
    solved[0] = first[:, size + TILE // 2 :]

    for copy in panel_copies[2]:
        copy.wait()

    def subtract(load, cols):
        for i in range(size // TILE):
            rows = slice(i * TILE, (i + 1) * TILE)
            change = jnp.dot(top[rows, :], first[:, cols], preferred_element_type=f32)
            updated[rows, cols] = (load(rows).astype(f32) - change).astype(bf16)

    @pl.loop(0, size // TILE)
    def _(t):
        subtract(lambda rows: tile(2, rows, t), at(t))

        def store(i, x):
            second[i * TILE : (i + 1) * TILE, at(t)] = x.astype(bf16)

        lower(1, lambda n: updated[:n, at(t)], store)

    subtract(lambda rows: side[1, rows, :], slice(size, size + TILE))

    def store_side_two(i, x):
        second[i * TILE : (i + 1) * TILE, size:] = x.astype(bf16)

    lower(1, lambda n: updated[:n, size:], store_side_two)
    solved[1] = second[:, size + TILE // 2 :]

    rows = pl.ds(pl.multiple_of(own, 16), factor.shape[1])
    factor[0] = first[rows, :size]
    factor[1] = second[rows, :size]

    for copy in late_copies:
        copy.wait()
    one = first[:, size:].T
    two = second[:, size:].T

    @pl.loop(0, size // TILE)
    def _(t):
        change = jnp.dot(one, first[:, at(t)], preferred_element_type=f32)
        change += jnp.dot(two, second[:, at(t)], preferred_element_type=f32)
        change = change.T
        trailing[at(t), :] = minuend[0, at(t), :].astype(f32) - change[:, : TILE // 2]
        residual[at(t), :] = minuend[1, at(t), :].astype(f32) - change[:, TILE // 2 :]


def exchange(blocks, axis):
    flat = blocks.reshape(blocks.shape[0], -1, blocks.shape[-1])
    return lax.all_to_all(flat, axis, 0, 0, tiled=True).reshape(blocks.shape)


def gather_small(block, axis, size):
    return exchange(jnp.broadcast_to(block[None], (size,) + block.shape), axis)


def shift(block, axis, size, by):
    return lax.ppermute(block, axis, [(i, (i + by) % size) for i in range(size)])


def call(body, name, outs, *operands):
    local = pl.BlockSpec(memory_space=pltpu.VMEM)
    return pl.pallas_call(
        body,
        name=name,
        out_shape=tuple(jax.ShapeDtypeStruct(shape, dtype) for shape, dtype in outs),
        in_specs=[local] * len(operands),
        out_specs=(local,) * len(outs),
        compiler_params=pltpu.CompilerParams(vmem_limit_bytes=2 << 20),
    )(*operands)


def stack(pieces):
    anywhere = pl.BlockSpec(memory_space=pl.ANY)
    return pl.pallas_call(
        stack_kernel,
        name="stack",
        out_shape=jax.ShapeDtypeStruct((len(pieces),) + pieces[0].shape, pieces[0].dtype),
        in_specs=[anywhere] * len(pieces),
        out_specs=anywhere,
        scratch_shapes=[pltpu.SemaphoreType.DMA((len(pieces),))],
        compiler_params=pltpu.CompilerParams(vmem_limit_bytes=1 << 20),
    )(*pieces)


def per_device(sizes, panel_top, panel_low, panel_next, gram_rest, inverses, right_top, right_low):
    rows, ys, cores, voxes = sizes
    axes = ("row", "y", "core", "vox")
    order = np.arange(rows * ys * cores * voxes).reshape(sizes)
    swap = list(zip(order.ravel().tolist(), order.transpose(1, 0, 2, 3).ravel().tolist()))
    y = lax.axis_index("y")
    core, vox = lax.axis_index("core"), lax.axis_index("vox")
    size, width = inverses.shape[2], panel_low.shape[1]
    cols = gram_rest.shape[1]
    bf16 = jnp.bfloat16
    other = [(0, 1), (1, 0)]

    own = ((y * cores + core) * voxes + vox) * width
    where = jnp.stack([y, core, own]).astype(jnp.int32)
    barrier = lax.optimization_barrier
    group = cores * voxes
    flats = [panel_low.T, panel_next.T]

    def ring(pieces, k, axis, n):
        up = pieces[k] = shift(pieces[k - 1], axis, n, 1)
        if k == n - k:
            return [up]
        down = pieces[n - k] = shift(pieces[(n - k + 1) % n], axis, n, -1)
        return [up, down]

    def ordered(values, pieces, k, n):
        keys = sorted({k, n - k})
        values, held = barrier((values, [pieces[i] for i in keys]))
        for i, piece in zip(keys, held):
            pieces[i] = piece
        return values

    whole = lax.all_gather(inverses, "row", axis=1, tiled=True)
    top = gather_small(panel_top.T, "row", rows)
    (sent,) = call(
        pack_kernel, "pack", [((cores, voxes, 3 * voxes + 2, width, cols), bf16)], top, *flats
    )
    got = exchange(sent.reshape((group,) + sent.shape[2:]), ("core", "vox"))
    mine, single = call(
        unpack_kernel, "unpack",
        [((3 * voxes, group, width, cols), bf16), ((group, 2, width, cols), bf16)], got,
    )
    pieces = {0: mine.reshape(3 * voxes, group * width, cols)}
    ring(pieces, 1, "y", ys)
    swapped = lax.ppermute(single, axes, swap)
    ring(pieces, 2, "y", ys)
    swapped = ordered(swapped, pieces, 2, ys)
    ring(pieces, 3, "y", ys)
    near = sorted(k % ys for k in range(-2, 3))
    far_near = lax.ppermute(stack([pieces[k] for k in near]), "core", other)
    matching = gather_small(swapped, "row", rows)
    far_near, whole = ordered((far_near, whole), pieces, 3, ys)
    ring(pieces, 4, "y", ys)
    rest = [pieces[k] for k in range(ys) if k not in near]
    far_rest = lax.ppermute(stack(rest), "core", other)

    matching = jnp.moveaxis(matching, 2, 0).reshape(2, size, cols)
    sides = [jnp.concatenate([matching[k], right_top[k]], axis=1) for k in range(2)]
    pieces = [pieces[k] for k in range(ys)]

    height = panel_low.shape[0]
    any_space = pl.BlockSpec(memory_space=pl.ANY)
    local = pl.BlockSpec(memory_space=pltpu.VMEM)
    vmem = pltpu.VMEM
    flops = 2 * size * size * (2 * size + TILE + 2 * (size + TILE) + 2 * TILE)
    factor, solved, trailing, residual = pl.pallas_call(
        functools.partial(factor_kernel, near, ys),
        out_shape=(
            jax.ShapeDtypeStruct((2, width, height), bf16),
            jax.ShapeDtypeStruct((2, size, cols), bf16),
            jax.ShapeDtypeStruct((height, cols), jnp.float32),
            jax.ShapeDtypeStruct((height, cols), jnp.float32),
        ),
        in_specs=[pl.BlockSpec(memory_space=pltpu.SMEM)] + [any_space] * (7 + ys),
        out_specs=(local,) * 4,
        scratch_shapes=[
            vmem((2, size, size), bf16),
            vmem((3, cores * voxes, ys, group * width, cols), bf16),
            vmem((2, size, TILE), bf16),
            vmem((2, height, cols), bf16),
            vmem((size, size), bf16),
            vmem((size, height + TILE), bf16),
            vmem((size, height + TILE), bf16),
            vmem((size, height + TILE), bf16),
            pltpu.SemaphoreType.DMA((6 * ys + 6,)),
        ],
        compiler_params=pltpu.CompilerParams(vmem_limit_bytes=56 * 1024 * 1024),
        cost_estimate=pl.CostEstimate(flops=flops, bytes_accessed=14 << 20, transcendentals=0),
        name="factor_and_update",
    )(where, whole, *pieces, far_near, far_rest, *sides, gram_rest, right_low)
    return (factor.transpose(0, 2, 1), solved, trailing, residual)


def solution(mesh):
    cores = 2
    sizes = (mesh.shape["row"], mesh.shape["col"] // cores, cores, mesh.shape["vox"])
    split = Mesh(mesh.devices.reshape(sizes), ("row", "y", "core", "vox"))
    cols = ("y", "core", "vox")
    in_specs = (
        P("row", cols),
        P("row", cols),
        P("row", cols),
        P("row", cols),
        P(None, "row", None),
        P(None, None, cols),
        P("row", cols),
    )
    out_specs = (
        P(None, "row", cols),
        P(None, None, cols),
        P("row", cols),
        P("row", cols),
    )
    return jax.shard_map(
        functools.partial(per_device, sizes),
        mesh=split,
        in_specs=in_specs,
        out_specs=out_specs,
        check_vma=False,
    )
```

```python
import functools

import jax
import jax.numpy as jnp
import numpy as np
from jax import lax
from jax.experimental import pallas as pl
from jax.experimental.pallas import tpu as pltpu
from jax.sharding import Mesh
from jax.sharding import PartitionSpec as P

BLOCK = 128


def factor_kernel(ys, at_ref, whole, *refs):
    pieces, others, refs = refs[:ys], refs[ys : 2 * ys], refs[2 * ys :]
    side_one, side_two, gram, right, factor, solved, trailing, residual = refs[:8]
    inv, head, panels, minuend, top, first, updated, second, sems = refs[8:]
    y, core, own = at_ref[0], at_ref[1], at_ref[2]
    size, wide = first.shape
    height = head.shape[-1]
    cols = gram.shape[1]
    f32, bf16 = jnp.float32, jnp.bfloat16

    panel_copies = [[], [], []]
    for p in range(3):
        target = head if p == 0 else panels.at[p - 1]
        for k in range(ys):
            spot = lax.rem(y + (ys - k), ys)
            for ref, half in ((pieces[k], core), (others[k], 1 - core)):
                panel_copies[p].append(
                    pltpu.make_async_copy(
                        ref.at[:, p],
                        target.at[spot, half, :, :, :height],
                        sems.at[2 * ys * p + len(panel_copies[p])],
                    )
                )
    rest_copies = [
        pltpu.make_async_copy(src, dst, sems.at[6 * ys + i])
        for i, (src, dst) in enumerate(
            (
                (whole.at[0], inv.at[0]),
                (whole.at[1], inv.at[1]),
                (side_one, panels.at[0, :, :, :, :, height:]),
                (side_two, panels.at[1, :, :, :, :, height:]),
                (gram, minuend.at[0]),
                (right, minuend.at[1]),
            )
        )
    ]
    groups = [
        rest_copies[:1] + panel_copies[0],
        panel_copies[1] + rest_copies[2:3],
        panel_copies[2] + rest_copies[3:4] + rest_copies[1:2],
        rest_copies[4:],
    ]
    for group in groups:
        for copy in group:
            copy.start()

    def wait(group):
        for copy in group:
            copy.wait()

    blocks = [slice(i * BLOCK, (i + 1) * BLOCK) for i in range(size // BLOCK)]

    def lower(k, right_of, i):
        n = (i + 1) * BLOCK
        return jnp.dot(inv[k, blocks[i], :n], right_of[:n, :], preferred_element_type=f32)

    flat_head = head.reshape(size, height)
    flat = panels.reshape(2, size, wide)

    wait(groups[0])
    for i, rows in enumerate(blocks):
        top[:, rows] = lower(0, flat_head, i).astype(bf16).T

    wait(groups[1])
    for i, rows in enumerate(blocks):
        first[rows, :] = lower(0, flat.at[0], i).astype(bf16)

    wait(groups[2])
    for rows in blocks:
        change = jnp.dot(top[rows, :], first[...], preferred_element_type=f32)
        updated[rows, :] = (flat[1, rows, :].astype(f32) - change).astype(bf16)
    for i, rows in enumerate(blocks):
        second[rows, :] = lower(1, updated, i).astype(bf16)

    solved[0] = first[:, height + cols :]
    solved[1] = second[:, height + cols :]
    mine = pl.ds(pl.multiple_of(own, 16), factor.shape[1])
    factor[0] = first[mine, :height]
    factor[1] = second[mine, :height]

    wait(groups[3])
    for j, out in enumerate((trailing, residual)):
        at = slice(height + j * cols, height + (j + 1) * cols)
        change = jnp.dot(first[:, at].T, first[:, :height], preferred_element_type=f32)
        change += jnp.dot(second[:, at].T, second[:, :height], preferred_element_type=f32)
        out[...] = minuend[j].astype(f32) - change.T


def gather_small(block, axis, size):
    flat = block.reshape(1, -1, block.shape[-1])
    out = lax.all_to_all(jnp.tile(flat, (size, 1, 1)), axis, 0, 0, tiled=True)
    return out.reshape((size,) + block.shape)


def shift(block, axis, size, by):
    return lax.ppermute(block, axis, [(i, (i + by) % size) for i in range(size)])


def per_device(sizes, panel_top, panel_low, panel_next, gram_rest, inverses, right_top, right_low):
    rows, ys, cores, voxes = sizes
    axes = ("row", "y", "core", "vox")
    order = np.arange(rows * ys * cores * voxes).reshape(sizes)
    swap = list(zip(order.ravel().tolist(), order.transpose(1, 0, 2, 3).ravel().tolist()))
    z, y = lax.axis_index("row"), lax.axis_index("y")
    core, vox = lax.axis_index("core"), lax.axis_index("vox")
    size, width = inverses.shape[2], panel_low.shape[1]
    cols = gram_rest.shape[1]
    bf16 = jnp.bfloat16
    other = [(0, 1), (1, 0)]

    whole = lax.all_gather(inverses, "row", axis=1, tiled=True)
    low, following = panel_low.T, panel_next.T
    pair = jnp.stack([low, following])
    swapped = lax.ppermute(pair, axes, swap)

    top = gather_small(panel_top.T, "row", rows).transpose(1, 0, 2).reshape(width, -1)
    top, swapped = lax.optimization_barrier((top, swapped))
    panels = gather_small(jnp.stack([top, low, following]), "vox", voxes)
    blocks = swapped.reshape(2, width, cores * voxes, cols).transpose(2, 0, 1, 3)

    up = down = panels
    pieces, others = {0: panels}, {}
    for k in range(1, ys // 2 + 1):
        if k == 2:
            up, down, blocks = lax.optimization_barrier((up, down, blocks))
        if k == 4:
            up, matching, whole = lax.optimization_barrier((up, matching, whole))
        if k == 1:
            blocks = lax.all_to_all(blocks, ("core", "vox"), 0, 0, tiled=True)
        if k == 2:
            matching = gather_small(blocks, "row", rows)
        pieces[k] = up = shift(up, "y", ys, 1)
        if k < ys - k:
            pieces[ys - k] = down = shift(down, "y", ys, -1)
    for k in range(ys):
        others[k] = lax.ppermute(pieces[k], "core", other)
    matching = jnp.moveaxis(matching, 2, 0)
    matching = matching.reshape(2, size, cols)
    sides = [jnp.concatenate([matching[k], right_top[k]], axis=1) for k in range(2)]
    sides = [side.reshape(ys, 2, voxes, width, 2 * cols) for side in sides]
    pieces = [pieces[k] for k in range(ys)]
    others = [others[k] for k in range(ys)]

    own = ((y * cores + core) * voxes + vox) * width
    where = jnp.stack([y, core, own]).astype(jnp.int32)
    height = panel_low.shape[0]
    any_space = pl.BlockSpec(memory_space=pl.ANY)
    local = pl.BlockSpec(memory_space=pltpu.VMEM)
    vmem = pltpu.VMEM
    flops = 2 * size * size * (4 * size + 10 * cols)
    factor, solved, trailing, residual = pl.pallas_call(
        functools.partial(factor_kernel, ys),
        out_shape=(
            jax.ShapeDtypeStruct((2, width, height), bf16),
            jax.ShapeDtypeStruct((2, size, cols), bf16),
            jax.ShapeDtypeStruct((height, cols), jnp.float32),
            jax.ShapeDtypeStruct((height, cols), jnp.float32),
        ),
        in_specs=[pl.BlockSpec(memory_space=pltpu.SMEM)] + [any_space] * (5 + 2 * ys),
        out_specs=(local,) * 4,
        scratch_shapes=[
            vmem((2, size, size), bf16),
            vmem((ys, cores, voxes, width, height), bf16),
            vmem((2, ys, cores, voxes, width, height + 2 * cols), bf16),
            vmem((2, height, cols), bf16),
            vmem((size, size), bf16),
            vmem((size, height + 2 * cols), bf16),
            vmem((size, height + 2 * cols), bf16),
            vmem((size, height + 2 * cols), bf16),
            pltpu.SemaphoreType.DMA((6 * ys + 6,)),
        ],
        compiler_params=pltpu.CompilerParams(vmem_limit_bytes=40 * 1024 * 1024),
        cost_estimate=pl.CostEstimate(flops=flops, bytes_accessed=14 << 20, transcendentals=0),
        name="factor_and_update",
    )(where, whole, *pieces, *others, *sides, gram_rest, right_low)
    return (factor.transpose(0, 2, 1), solved, trailing, residual)


def solution(mesh):
    cores = 2
    sizes = (mesh.shape["row"], mesh.shape["col"] // cores, cores, mesh.shape["vox"])
    split = Mesh(mesh.devices.reshape(sizes), ("row", "y", "core", "vox"))
    cols = ("y", "core", "vox")
    in_specs = (
        P("row", cols),
        P("row", cols),
        P("row", cols),
        P("row", cols),
        P(None, "row", None),
        P(None, None, cols),
        P("row", cols),
    )
    out_specs = (
        P(None, "row", cols),
        P(None, None, cols),
        P("row", cols),
        P("row", cols),
    )
    return jax.shard_map(
        functools.partial(per_device, sizes),
        mesh=split,
        in_specs=in_specs,
        out_specs=out_specs,
        check_vma=False,
    )
```

```python
import functools

import jax
import jax.numpy as jnp
import numpy as np
from jax import lax
from jax.experimental import pallas as pl
from jax.experimental.pallas import tpu as pltpu
from jax.sharding import Mesh
from jax.sharding import PartitionSpec as P

BLOCK = 128


def factor_kernel(ys, near, rest, at_ref, whole, *refs):
    pieces, far_near, far_rest, refs = refs[:ys], refs[ys], refs[ys + 1], refs[ys + 2 :]
    others = {k: far_near.at[i] for i, k in enumerate(near)}
    others |= {k: far_rest.at[i] for i, k in enumerate(rest)}
    side_one, side_two, gram, right, factor, solved, trailing, residual = refs[:8]
    inv, head, panels, minuend, top, first, updated, second, sems = refs[8:]
    y, core, own = at_ref[0], at_ref[1], at_ref[2]
    size, wide = first.shape
    height = head.shape[-1]
    cols = gram.shape[1]
    f32, bf16 = jnp.float32, jnp.bfloat16

    panel_copies = [[], [], []]
    for p in range(3):
        target = head if p == 0 else panels.at[p - 1]
        for k in range(ys):
            spot = lax.rem(y + (ys - k), ys)
            for ref, half in ((pieces[k], core), (others[k], 1 - core)):
                panel_copies[p].append(
                    pltpu.make_async_copy(
                        ref.at[:, p],
                        target.at[spot, half, :, :, :height],
                        sems.at[2 * ys * p + len(panel_copies[p])],
                    )
                )
    rest_copies = [
        pltpu.make_async_copy(src, dst, sems.at[6 * ys + i])
        for i, (src, dst) in enumerate(
            (
                (whole.at[0], inv.at[0]),
                (whole.at[1], inv.at[1]),
                (side_one, panels.at[0, :, :, :, :, height:]),
                (side_two, panels.at[1, :, :, :, :, height:]),
                (gram, minuend.at[0]),
                (right, minuend.at[1]),
            )
        )
    ]
    groups = [
        rest_copies[:1] + panel_copies[0],
        panel_copies[1] + rest_copies[2:3],
        panel_copies[2] + rest_copies[3:4] + rest_copies[1:2],
        rest_copies[4:],
    ]
    for group in groups:
        for copy in group:
            copy.start()

    def wait(group):
        for copy in group:
            copy.wait()

    blocks = [slice(i * BLOCK, (i + 1) * BLOCK) for i in range(size // BLOCK)]

    def lower(k, right_of, i):
        n = (i + 1) * BLOCK
        return jnp.dot(inv[k, blocks[i], :n], right_of[:n, :], preferred_element_type=f32)

    flat_head = head.reshape(size, height)
    flat = panels.reshape(2, size, wide)

    wait(groups[0])
    for i, rows in enumerate(blocks):
        top[:, rows] = lower(0, flat_head, i).astype(bf16).T

    wait(groups[1])
    for i, rows in enumerate(blocks):
        first[rows, :] = lower(0, flat.at[0], i).astype(bf16)

    wait(groups[2])
    for rows in blocks:
        change = jnp.dot(top[rows, :], first[...], preferred_element_type=f32)
        updated[rows, :] = (flat[1, rows, :].astype(f32) - change).astype(bf16)
    for i, rows in enumerate(blocks):
        second[rows, :] = lower(1, updated, i).astype(bf16)

    solved[0] = first[:, height + cols :]
    solved[1] = second[:, height + cols :]
    mine = pl.ds(pl.multiple_of(own, 16), factor.shape[1])
    factor[0] = first[mine, :height]
    factor[1] = second[mine, :height]

    wait(groups[3])
    for j, out in enumerate((trailing, residual)):
        at = slice(height + j * cols, height + (j + 1) * cols)
        change = jnp.dot(first[:, at].T, first[:, :height], preferred_element_type=f32)
        change += jnp.dot(second[:, at].T, second[:, :height], preferred_element_type=f32)
        out[...] = minuend[j].astype(f32) - change.T


def gather_small(block, axis, size):
    flat = block.reshape(1, -1, block.shape[-1])
    out = lax.all_to_all(jnp.tile(flat, (size, 1, 1)), axis, 0, 0, tiled=True)
    return out.reshape((size,) + block.shape)


def stack_kernel(*refs):
    pieces, stacked, sems = refs[:-2], refs[-2], refs[-1]
    copies = [
        pltpu.make_async_copy(ref, stacked.at[i], sems.at[i]) for i, ref in enumerate(pieces)
    ]
    for copy in copies:
        copy.start()
    for copy in copies:
        copy.wait()


def stack(pieces):
    anywhere = pl.BlockSpec(memory_space=pl.ANY)
    return pl.pallas_call(
        stack_kernel,
        name="stack",
        out_shape=jax.ShapeDtypeStruct((len(pieces),) + pieces[0].shape, pieces[0].dtype),
        in_specs=[anywhere] * len(pieces),
        out_specs=anywhere,
        scratch_shapes=[pltpu.SemaphoreType.DMA((len(pieces),))],
        compiler_params=pltpu.CompilerParams(vmem_limit_bytes=1 << 20),
    )(*pieces)


def shift(block, axis, size, by):
    return lax.ppermute(block, axis, [(i, (i + by) % size) for i in range(size)])


def per_device(sizes, panel_top, panel_low, panel_next, gram_rest, inverses, right_top, right_low):
    rows, ys, cores, voxes = sizes
    axes = ("row", "y", "core", "vox")
    order = np.arange(rows * ys * cores * voxes).reshape(sizes)
    swap = list(zip(order.ravel().tolist(), order.transpose(1, 0, 2, 3).ravel().tolist()))
    z, y = lax.axis_index("row"), lax.axis_index("y")
    core, vox = lax.axis_index("core"), lax.axis_index("vox")
    size, width = inverses.shape[2], panel_low.shape[1]
    cols = gram_rest.shape[1]
    bf16 = jnp.bfloat16
    other = [(0, 1), (1, 0)]

    whole = lax.all_gather(inverses, "row", axis=1, tiled=True)
    low, following = panel_low.T, panel_next.T
    pair = jnp.stack([low, following])
    swapped = lax.ppermute(pair, axes, swap)

    top = gather_small(panel_top.T, "row", rows).transpose(1, 0, 2).reshape(width, -1)
    top, swapped = lax.optimization_barrier((top, swapped))
    panels = gather_small(jnp.stack([top, low, following]), "vox", voxes)
    blocks = swapped.reshape(2, width, cores * voxes, cols).transpose(2, 0, 1, 3)

    up = down = panels
    pieces = {0: panels}
    for k in range(1, ys // 2 + 1):
        if k == 2:
            up, down, blocks = lax.optimization_barrier((up, down, blocks))
        if k == 4:
            up, matching, whole = lax.optimization_barrier((up, matching, whole))
        if k == 1:
            blocks = lax.all_to_all(blocks, ("core", "vox"), 0, 0, tiled=True)
        if k == 2:
            matching = gather_small(blocks, "row", rows)
        pieces[k] = up = shift(up, "y", ys, 1)
        if k < ys - k:
            pieces[ys - k] = down = shift(down, "y", ys, -1)
        if k == 3:
            near = sorted(j % ys for j in range(-2, 3))
            far_near = lax.ppermute(stack([pieces[j] for j in near]), "core", other)
    rest = [k for k in range(ys) if k not in near]
    far_rest = lax.ppermute(stack([pieces[k] for k in rest]), "core", other)
    matching = jnp.moveaxis(matching, 2, 0)
    matching = matching.reshape(2, size, cols)
    sides = [jnp.concatenate([matching[k], right_top[k]], axis=1) for k in range(2)]
    sides = [side.reshape(ys, 2, voxes, width, 2 * cols) for side in sides]
    pieces = [pieces[k] for k in range(ys)]

    own = ((y * cores + core) * voxes + vox) * width
    where = jnp.stack([y, core, own]).astype(jnp.int32)
    height = panel_low.shape[0]
    any_space = pl.BlockSpec(memory_space=pl.ANY)
    local = pl.BlockSpec(memory_space=pltpu.VMEM)
    vmem = pltpu.VMEM
    flops = 2 * size * size * (4 * size + 10 * cols)
    factor, solved, trailing, residual = pl.pallas_call(
        functools.partial(factor_kernel, ys, near, rest),
        out_shape=(
            jax.ShapeDtypeStruct((2, width, height), bf16),
            jax.ShapeDtypeStruct((2, size, cols), bf16),
            jax.ShapeDtypeStruct((height, cols), jnp.float32),
            jax.ShapeDtypeStruct((height, cols), jnp.float32),
        ),
        in_specs=[pl.BlockSpec(memory_space=pltpu.SMEM)] + [any_space] * (7 + ys),
        out_specs=(local,) * 4,
        scratch_shapes=[
            vmem((2, size, size), bf16),
            vmem((ys, cores, voxes, width, height), bf16),
            vmem((2, ys, cores, voxes, width, height + 2 * cols), bf16),
            vmem((2, height, cols), bf16),
            vmem((size, size), bf16),
            vmem((size, height + 2 * cols), bf16),
            vmem((size, height + 2 * cols), bf16),
            vmem((size, height + 2 * cols), bf16),
            pltpu.SemaphoreType.DMA((6 * ys + 6,)),
        ],
        compiler_params=pltpu.CompilerParams(vmem_limit_bytes=56 * 1024 * 1024),
        cost_estimate=pl.CostEstimate(flops=flops, bytes_accessed=14 << 20, transcendentals=0),
        name="factor_and_update",
    )(where, whole, *pieces, far_near, far_rest, *sides, gram_rest, right_low)
    return (factor.transpose(0, 2, 1), solved, trailing, residual)


def solution(mesh):
    cores = 2
    sizes = (mesh.shape["row"], mesh.shape["col"] // cores, cores, mesh.shape["vox"])
    split = Mesh(mesh.devices.reshape(sizes), ("row", "y", "core", "vox"))
    cols = ("y", "core", "vox")
    in_specs = (
        P("row", cols),
        P("row", cols),
        P("row", cols),
        P("row", cols),
        P(None, "row", None),
        P(None, None, cols),
        P("row", cols),
    )
    out_specs = (
        P(None, "row", cols),
        P(None, None, cols),
        P("row", cols),
        P("row", cols),
    )
    return jax.shard_map(
        functools.partial(per_device, sizes),
        mesh=split,
        in_specs=in_specs,
        out_specs=out_specs,
        check_vma=False,
    )
```
